32 devices in a mesh: grp: 8 (over z, core), row: 4 (over y, x).
Axes of the slice: x: 2, y: 2, z: 4, core: 2. Of those that a mesh axis runs over, the one named last changes fastest.
Arguments:
- panel_low: bfloat16 [32768, 256], P(('grp', 'row')), may hold values from -6 to 6
- panel_mid: bfloat16 [16384, 256], P(('grp', 'row')), may hold values from -6 to 6
- panel_top: bfloat16 [8192, 256], P(('grp', 'row')), may hold values from -6 to 6
- inverse_low: bfloat16 [2, 32768, 4096], P(None, ('grp', 'row')), may hold values from -0.0625 to 0.0625
- inverse_mid: bfloat16 [2, 16384, 4096], P(None, ('grp', 'row')), may hold values from -0.0625 to 0.0625
- inverse_top: bfloat16 [2, 8192, 4096], P(None, ('grp', 'row')), may hold values from -0.0625 to 0.0625
- couple_low: bfloat16 [2, 2048, 32768], P(None, None, ('grp', 'row')), may hold values from -0.0625 to 0.0625
- couple_mid: bfloat16 [2, 2048, 16384], P(None, None, ('grp', 'row')), may hold values from -0.0625 to 0.0625
- parents_low: int32 [8, 2048], replicated, may hold values from 0 to 4095, as said below
- parents_mid: int32 [4, 2048], replicated, may hold values from 0 to 4095, as said below
Outputs:
- solution_low: float32 [32768, 256], P(('grp', 'row'))
- solution_mid: float32 [16384, 256], P(('grp', 'row'))
- solution_top: float32 [8192, 256], P(('grp', 'row'))
The draws below stay inside these ranges and needn't reach their ends.
Inputs may be any that keep to these rules, and one draw needn't show every extreme that they name: `parents_low`: each row holds 2048 distinct row numbers of the parent front. `parents_mid`: each row holds 2048 distinct row numbers of the parent front.
All inputs are finite; a program needn't handle non-finite values.
Results may differ from the reference program's by a relative error of at most 0.024.
Values may be sent and summed in bfloat16 or wider, within the bound.
A program may use at most 128 MiB of HBM per device.

```python
import jax
import jax.numpy as jnp
from jax import lax

F = 4096
K = 2048
R = 128
NLOW = 8
NMID = 4
NTOP = 2


def target_rows(key, count):

    def one_front(front_key):
        key_hot, key_score = jax.random.split(front_key)
        hot_blocks = jax.random.randint(key_hot, (16,), 0, 2)
        weights = 1 + 3 * jnp.repeat(hot_blocks, F // 16)
        scores = jax.random.randint(key_score, (F,), 0, 1024) * weights
        order = jnp.argsort(-(scores * F + jnp.arange(F)))
        return order[:K].astype(jnp.int32)
    keys = jax.random.split(key, count)
    rows = jax.vmap(one_front)(keys)
    chosen = jax.random.randint(jax.random.fold_in(key, 7), (), 0, count)
    ends = jnp.array([F - 1, 0], dtype=jnp.int32)
    middle = 1 + jax.random.permutation(jax.random.fold_in(key, 11), F - 2).astype(jnp.int32)
    forced = jnp.concatenate([ends, middle[:K - 2]])
    forced = jax.random.permutation(jax.random.fold_in(key, 13), forced)
    rows = jnp.where(jnp.arange(count)[:, None] == chosen, forced[None, :], rows)
    return rows.astype(jnp.int32)


def draw_parents_low(key, part):
    return target_rows(jax.random.fold_in(key, 101), NLOW)


def draw_parents_mid(key, part):
    return target_rows(jax.random.fold_in(key, 202), NMID)


def levels(rng, extent, pieces, low, largest):
    gain = 1.0
    for dim, shards_of in pieces:
        steps = jax.random.uniform(jax.random.fold_in(jax.random.fold_in(rng, 6), dim), (shards_of,), jnp.float32, low / len(pieces), largest / len(pieces))
        gain = gain * jnp.repeat(jnp.exp(steps), extent[dim] // shards_of).reshape((-1,) + (1,) * (len(extent) - 1 - dim))
    return gain


def normal_values(key, dims, scale, limit, shards=(), kind=jnp.bfloat16):
    factor_of = levels(key, dims, shards, -0.22, 0.18) if shards else 1.0
    result = jax.random.normal(key, dims, jnp.float32) * scale * factor_of
    return jnp.minimum(jnp.maximum(result, -limit), limit).astype(kind)


def setup_inputs(seed: int = 0) -> dict:
    streams_of = jax.random.split(jax.random.key(seed), 11)
    panel_low = normal_values(streams_of[0], (NLOW * F, 2 * R), 1.0, 6.0, ((0, 32),))
    panel_mid = normal_values(streams_of[1], (NMID * F, 2 * R), 1.0, 6.0, ((0, 32),))
    panel_top = normal_values(streams_of[2], (NTOP * F, 2 * R), 1.0, 6.0, ((0, 32),))
    inverse_low = normal_values(streams_of[3], (2, NLOW * F, F), (2 * F) ** -0.5, 0.0625, ((1, 32),))
    inverse_mid = normal_values(streams_of[4], (2, NMID * F, F), (2 * F) ** -0.5, 0.0625, ((1, 32),))
    inverse_top = normal_values(streams_of[5], (2, NTOP * F, F), (2 * F) ** -0.5, 0.0625, ((1, 32),))
    couple_low = normal_values(streams_of[6], (2, K, NLOW * F), (2 * F) ** -0.5, 0.0625, ((2, 32),))
    couple_mid = normal_values(streams_of[7], (2, K, NMID * F), (2 * F) ** -0.5, 0.0625, ((2, 32),))
    parents_low = draw_parents_low(jax.random.fold_in(streams_of[10], 71), 0)
    parents_mid = draw_parents_mid(jax.random.fold_in(streams_of[10], 71), 0)
    return {"panel_low": panel_low, "panel_mid": panel_mid, "panel_top": panel_top, "inverse_low": inverse_low, "inverse_mid": inverse_mid, "inverse_top": inverse_top, "couple_low": couple_low, "couple_mid": couple_mid, "parents_low": parents_low, "parents_mid": parents_mid}


def complex_product(matrix, panel):
    width = panel.shape[1] // 2
    real_term = jnp.dot(matrix[0], panel, preferred_element_type=jnp.float32)
    imag_term = jnp.dot(matrix[1], panel, preferred_element_type=jnp.float32)
    return real_term + jnp.concatenate([-imag_term[:, width:], imag_term[:, :width]], axis=1)


def transposed_product(matrix, panel):
    width = panel.shape[1] // 2
    real_term = jnp.dot(matrix[0].T, panel, preferred_element_type=jnp.float32)
    imag_term = jnp.dot(matrix[1].T, panel, preferred_element_type=jnp.float32)
    return real_term + jnp.concatenate([-imag_term[:, width:], imag_term[:, :width]], axis=1)


def split_inverse(matrix, count):
    return matrix.reshape(2, count, F, F).transpose(1, 0, 2, 3)


def split_couple(matrix, count):
    return matrix.reshape(2, K, count, F).transpose(2, 0, 1, 3)


def solve_each(pair):
    return complex_product(pair[0], pair[1])


def assemble(parent_panel, parts, targets, count):
    def scatter_one(pair):
        return jnp.zeros((F, 2 * R), jnp.float32).at[pair[0]].add(pair[1])

    spread = lax.map(scatter_one, (targets, parts))
    summed = spread.reshape(count, 2, F, 2 * R).sum(axis=1)
    return (parent_panel.astype(jnp.float32) - summed).astype(jnp.bfloat16)


def descend(parent_x, targets, couples, inverses, own_y):
    upper = jnp.repeat(parent_x.astype(jnp.bfloat16), 2, axis=0)

    def one_front(items):
        up_panel, rows, couple, inverse, own = items
        picked = up_panel[rows]
        lifted = transposed_product(couple, picked).astype(jnp.bfloat16)
        return own - complex_product(inverse, lifted)

    return lax.map(one_front, (upper, targets, couples, inverses, own_y))


def reference(panel_low, panel_mid, panel_top, inverse_low, inverse_mid, inverse_top, couple_low, couple_mid, parents_low, parents_mid):
    inv_lowest = split_inverse(inverse_low, NLOW)
    inv_middle = split_inverse(inverse_mid, NMID)
    inv_upper = split_inverse(inverse_top, NTOP)
    cpl_lowest = split_couple(couple_low, NLOW)
    cpl_middle = split_couple(couple_mid, NMID)
    low_y = lax.map(solve_each, (inv_lowest, panel_low.reshape(NLOW, F, 2 * R)))
    low_part = lax.map(solve_each, (cpl_lowest, low_y.astype(jnp.bfloat16)))
    mid_right = assemble(panel_mid.reshape(NMID, F, 2 * R), low_part, parents_low, NMID)
    mid_y = lax.map(solve_each, (inv_middle, mid_right))
    mid_part = lax.map(solve_each, (cpl_middle, mid_y.astype(jnp.bfloat16)))
    top_right = assemble(panel_top.reshape(NTOP, F, 2 * R), mid_part, parents_mid, NTOP)
    top_x = lax.map(solve_each, (inv_upper, top_right))
    mid_x = descend(top_x, parents_mid, cpl_middle, inv_middle, mid_y)
    low_x = descend(mid_x, parents_low, cpl_lowest, inv_lowest, low_y)
    return (low_x.reshape(NLOW * F, 2 * R), mid_x.reshape(NMID * F, 2 * R), top_x.reshape(NTOP * F, 2 * R))
```

```python
import functools

import jax
import jax.numpy as jnp
from jax import lax
from jax.experimental import pallas as pl
from jax.experimental.pallas import tpu as pltpu
from jax.sharding import PartitionSpec as P

F = 4096
MESH = pl.DeviceIdType.MESH


def complex_product(matrix, panel):
    width = panel.shape[1] // 2
    real_term = jnp.dot(matrix[0], panel, preferred_element_type=jnp.float32)
    imag_term = jnp.dot(matrix[1], panel, preferred_element_type=jnp.float32)
    return real_term + jnp.concatenate([-imag_term[:, width:], imag_term[:, :width]], axis=1)


def transposed_product(matrix, panel):
    width = panel.shape[1] // 2
    contract = (((0,), (0,)), ((), ()))
    real_term = lax.dot_general(matrix[0], panel, contract, preferred_element_type=jnp.float32)
    imag_term = lax.dot_general(matrix[1], panel, contract, preferred_element_type=jnp.float32)
    return real_term + jnp.concatenate([-imag_term[:, width:], imag_term[:, :width]], axis=1)


class Place:
    def __init__(self, n, levels):
        self.n = n
        self.levels = levels
        self.group = lax.axis_index("grp")
        self.row = lax.axis_index("row")
        self.core = lax.rem(self.group, 2)
        self.upper = lax.rem(self.group // 2, 2)
        self.partner = (self.group + 1 - 2 * self.core, self.row)
        self.across = (self.group + 2 - 4 * self.upper, self.row)
        self.unit = lax.rem(self.group, 2**levels)

    def ahead(self, step):
        return lax.rem(self.row + step, self.n)

    def behind(self, step):
        return lax.rem(self.row + self.n - step, self.n)

    def greet(self):
        barrier = pltpu.get_barrier_semaphore()
        peers = [(self.group, self.ahead(s)) for s in range(1, self.n)]
        if self.levels >= 1:
            peers.append(self.partner)
        if self.levels >= 2:
            peers.append(self.across)
        for peer in peers:
            pl.semaphore_signal(barrier, inc=1, device_id=peer, device_id_type=MESH)
        pl.semaphore_wait(barrier, len(peers))


def push(src, dst, send, recv, peer):
    return pltpu.make_async_remote_copy(
        src_ref=src, dst_ref=dst, send_sem=send, recv_sem=recv, device_id=peer, device_id_type=MESH
    )


def spread(at, own, out, sems):
    n, levels = at.n, at.levels
    row_send, row_recv, pair_send, pair_recv, z_send, z_recv = sems
    near = at.unit
    started = []

    def to_rows(which, unit):
        src = out.at[unit * n + at.row]
        for s in range(1, n):
            copy = push(src, src, row_send.at[which, s], row_recv.at[which, s], (at.group, at.ahead(s)))
            copy.start()
            started.append(copy)

    def to_pair(which, index, unit, row):
        src = out.at[unit * n + row]
        copy = push(src, src, pair_send.at[which, index], pair_recv.at[which, index], at.partner)
        copy.start()
        started.append(copy)

    units = [near]
    if levels >= 2:
        far = lax.rem(near + 2, 4)
        units.append(far)
        src = out.at[near * n + at.row]
        z_copy = push(src, src, z_send.at[0], z_recv.at[0], at.across)
        z_copy.start()
        started.append(z_copy)
    to_rows(0, near)
    if levels >= 1:
        to_pair(0, 0, near, at.row)
    if levels >= 2:
        landed = out.at[units[1] * n + at.row]
        push(landed, landed, z_send.at[0], z_recv.at[0], at.across).wait_recv()
        to_rows(1, units[1])
        to_pair(1, 0, units[1], at.row)
    for which, unit in enumerate(units):
        for s in range(1, n):
            landed = out.at[unit * n + at.behind(s)]
            push(
                landed, landed, row_send.at[which, s], row_recv.at[which, s], (at.group, at.behind(s))
            ).wait_recv()
            if levels >= 1:
                to_pair(which, s, unit, at.behind(s))
    if levels >= 1:
        for which, unit in enumerate(units):
            other = unit + 1 - 2 * at.core
            for s in range(n):
                landed = out.at[other * n + at.behind(s)]
                push(
                    landed, landed, pair_send.at[which, s], pair_recv.at[which, s], at.partner
                ).wait_recv()
    for copy in started:
        copy.wait_send()


def gather_kernel(n, levels, own, out, *sems):
    at = Place(n, levels)
    at.greet()
    slot = at.unit * n + at.row
    out[slot] = own[...]
    spread(at, own, out, sems)


def add_rows(out_ref, terms, panel=None):
    rows = out_ref.shape[0]
    step = min(rows, 64)

    def body(index, carry):
        span = pl.ds(pl.multiple_of(index * step, step), step)
        total = terms[0][span, :].astype(jnp.float32)
        for term in terms[1:]:
            total = total + term[span, :].astype(jnp.float32)
        if panel is not None:
            total = panel[span, :].astype(jnp.float32) - total
        out_ref[span, :] = total.astype(out_ref.dtype)
        return carry

    lax.fori_loop(0, rows // step, body, 0)


def reduce_kernel(n, levels, term, panel, out, near_buf, stage, row_buf, z_stage, z_buf, *sems):
    at = Place(n, levels)
    halves = 2 ** (levels - 1)
    spread_sems = sems[:6]
    pair_send, pair_recv, row_send, row_recv, z_send, z_recv = sems[6:]
    at.greet()
    started = []
    for s in list(range(1, n)) + [0]:
        for half in range(halves):
            t = at.ahead(s)
            src = term.at[(half * 2 + 1 - at.core) * n + t]
            copy = push(
                src, near_buf.at[half, s], pair_send.at[half, s], pair_recv.at[half, s], at.partner
            )
            copy.start()
            started.append(copy)
    for s in range(1, n):
        for half in range(halves):
            t = at.ahead(s)
            landed = near_buf.at[half, s]
            push(
                landed, landed, pair_send.at[half, s], pair_recv.at[half, s], at.partner
            ).wait_recv()
            add_rows(stage.at[half, s], [term.at[(half * 2 + at.core) * n + t], landed])
            copy = push(
                stage.at[half, s],
                row_buf.at[half, s],
                row_send.at[half, s],
                row_recv.at[half, s],
                (at.group, t),
            )
            copy.start()
            started.append(copy)
    for half in range(halves):
        landed = near_buf.at[half, 0]
        push(landed, landed, pair_send.at[half, 0], pair_recv.at[half, 0], at.partner).wait_recv()
    for half in range(halves):
        for s in range(1, n):
            landed = row_buf.at[half, s]
            push(
                landed, landed, row_send.at[half, s], row_recv.at[half, s], (at.group, at.behind(s))
            ).wait_recv()

    def terms_of(half):
        own = term.at[(half * 2 + at.core) * n + at.row]
        return [own, near_buf.at[half, 0]] + [row_buf.at[half, s] for s in range(1, n)]

    slot = at.unit * n + at.row
    if levels == 1:
        add_rows(out.at[slot], terms_of(0), panel)
    else:
        add_rows(z_stage, terms_of(1 - at.upper))
        copy = push(z_stage, z_buf, z_send.at[0], z_recv.at[0], at.across)
        copy.start()
        started.append(copy)
        push(z_buf, z_buf, z_send.at[0], z_recv.at[0], at.across).wait_recv()
        add_rows(out.at[slot], terms_of(at.upper) + [z_buf], panel)
    spread(at, None, out, spread_sems)
    for copy in started:
        copy.wait_send()


def dma(*shape):
    return pltpu.SemaphoreType.DMA(shape)


def spread_scratch(n):
    return [dma(2, n), dma(2, n), dma(2, n), dma(2, n), dma(1), dma(1)]


def gather(own, n, levels, ident):
    block, width = own.shape
    count = 2**levels * n
    vmem = pl.BlockSpec(memory_space=pltpu.VMEM)
    full = pl.pallas_call(
        functools.partial(gather_kernel, n, levels),
        out_shape=jax.ShapeDtypeStruct((count, block, width), own.dtype),
        in_specs=[vmem],
        out_specs=vmem,
        scratch_shapes=spread_scratch(n),
        compiler_params=pltpu.CompilerParams(
            collective_id=ident, has_side_effects=True, vmem_limit_bytes=16 << 20
        ),
    )(own)
    return full.reshape(count * block, width)


def reduce_all(term, panel, n, levels, ident):
    block, width = panel.shape
    count = 2**levels * n
    halves = 2 ** (levels - 1)
    vmem = pl.BlockSpec(memory_space=pltpu.VMEM)
    buffers = pltpu.VMEM((halves, n, block, width), jnp.bfloat16)
    single = pltpu.VMEM((block, width), jnp.bfloat16)
    full = pl.pallas_call(
        functools.partial(reduce_kernel, n, levels),
        out_shape=jax.ShapeDtypeStruct((count, block, width), jnp.bfloat16),
        in_specs=[vmem, vmem],
        out_specs=vmem,
        scratch_shapes=[buffers, buffers, buffers, single, single]
        + spread_scratch(n)
        + [dma(halves, n), dma(halves, n), dma(halves, n), dma(halves, n), dma(1), dma(1)],
        compiler_params=pltpu.CompilerParams(
            collective_id=ident, has_side_effects=True, vmem_limit_bytes=24 << 20
        ),
    )(term.reshape(count, block, width), panel)
    return full.reshape(count * block, width)


def spread_rows(partial_rows, targets):
    marks = (lax.broadcasted_iota(jnp.int32, (F, 1), 0) == targets[None, :]).astype(jnp.bfloat16)
    return jnp.dot(
        marks, partial_rows.astype(jnp.bfloat16), preferred_element_type=jnp.float32
    ).astype(jnp.bfloat16)


def pick_rows(panel, targets):
    marks = (targets[:, None] == lax.broadcasted_iota(jnp.int32, (1, F), 1)).astype(jnp.bfloat16)
    return jnp.dot(marks, panel, preferred_element_type=jnp.float32).astype(jnp.bfloat16)


def on_device(
    n,
    panel_low,
    panel_mid,
    panel_top,
    inverse_low,
    inverse_mid,
    inverse_top,
    couple_low,
    couple_mid,
    parents_low,
    parents_mid,
):
    group = lax.axis_index("grp")
    low_targets = lax.dynamic_index_in_dim(parents_low, group, 0, keepdims=False)
    mid_targets = lax.dynamic_index_in_dim(parents_mid, group // 2, 0, keepdims=False)
    low_y = complex_product(inverse_low, gather(panel_low, n, 0, 0))
    term = spread_rows(complex_product(couple_low, low_y.astype(jnp.bfloat16)), low_targets)
    mid_y = complex_product(inverse_mid, reduce_all(term, panel_mid, n, 1, 1))
    term = spread_rows(complex_product(couple_mid, mid_y.astype(jnp.bfloat16)), mid_targets)
    top_x = complex_product(inverse_top, reduce_all(term, panel_top, n, 2, 2))
    top_full = gather(top_x.astype(jnp.bfloat16), n, 2, 3)
    lift = transposed_product(couple_mid, pick_rows(top_full, mid_targets)).astype(jnp.bfloat16)
    mid_x = mid_y - complex_product(inverse_mid, gather(lift, n, 1, 4))
    mid_full = gather(mid_x.astype(jnp.bfloat16), n, 1, 5)
    lift = transposed_product(couple_low, pick_rows(mid_full, low_targets)).astype(jnp.bfloat16)
    low_x = low_y - complex_product(inverse_low, gather(lift, n, 0, 6))
    return (low_x, mid_x, top_x)


def solution(mesh):
    placed = (
        P(("grp", "row"), None),
        P(("grp", "row"), None),
        P(("grp", "row"), None),
        P(None, ("grp", "row"), None),
        P(None, ("grp", "row"), None),
        P(None, ("grp", "row"), None),
        P(None, None, ("grp", "row")),
        P(None, None, ("grp", "row")),
        P(),
        P(),
    )
    return jax.shard_map(
        functools.partial(on_device, mesh.shape["row"]),
        mesh=mesh,
        in_specs=placed,
        out_specs=(P(("grp", "row"), None), P(("grp", "row"), None), P(("grp", "row"), None)),
        check_vma=False,
    )
```

```python
import functools

import jax
import jax.numpy as jnp
from jax import lax
from jax.experimental import pallas as pl
from jax.experimental.pallas import tpu as pltpu
from jax.sharding import PartitionSpec as P

F = 4096
MESH = pl.DeviceIdType.MESH


def complex_product(matrix, panel):
    width = panel.shape[1] // 2
    real_term = jnp.dot(matrix[0], panel, preferred_element_type=jnp.float32)
    imag_term = jnp.dot(matrix[1], panel, preferred_element_type=jnp.float32)
    return real_term + jnp.concatenate([-imag_term[:, width:], imag_term[:, :width]], axis=1)


def transposed_product(matrix, panel):
    width = panel.shape[1] // 2
    contract = (((0,), (0,)), ((), ()))
    real_term = lax.dot_general(matrix[0], panel, contract, preferred_element_type=jnp.float32)
    imag_term = lax.dot_general(matrix[1], panel, contract, preferred_element_type=jnp.float32)
    return real_term + jnp.concatenate([-imag_term[:, width:], imag_term[:, :width]], axis=1)


class Place:
    def __init__(self, n, levels):
        self.n = n
        self.levels = levels
        self.square = n == 4
        self.group = lax.axis_index("grp")
        self.row = lax.axis_index("row")
        self.core = lax.rem(self.group, 2)
        self.upper = lax.rem(self.group // 2, 2)
        self.partner = (self.group + 1 - 2 * self.core, self.row)
        self.across = (self.group + 2 - 4 * self.upper, self.row)
        self.unit = lax.rem(self.group, 2**levels)
        if self.square:
            side = self.row + 1 - 2 * lax.rem(self.row, 2)
            over = self.row + 2 - 4 * (self.row // 2)
            self.ring = [self.row, side, over, 3 - self.row]
            self.side = (self.group, side)
            self.over = (self.group, over)

    def ahead(self, step):
        return self.ring[step] if self.square else lax.rem(self.row + step, self.n)

    def behind(self, step):
        return self.ring[step] if self.square else lax.rem(self.row + self.n - step, self.n)

    def greet(self):
        barrier = pltpu.get_barrier_semaphore()
        if self.square:
            peers = [self.side, self.over]
        else:
            peers = [(self.group, self.ahead(s)) for s in range(1, self.n)]
        if self.levels >= 1:
            peers.append(self.partner)
        if self.levels >= 2:
            peers.append(self.across)
        for peer in peers:
            pl.semaphore_signal(barrier, inc=1, device_id=peer, device_id_type=MESH)
        pl.semaphore_wait(barrier, len(peers))


def push(src, dst, send, recv, peer):
    return pltpu.make_async_remote_copy(
        src_ref=src, dst_ref=dst, send_sem=send, recv_sem=recv, device_id=peer, device_id_type=MESH
    )


def half_of(ref, index):
    rows = ref.shape[0] // 2
    return ref.at[pl.ds(index * rows, rows)]


def spread(at, out, sems, use):
    n, levels = at.n, at.levels
    row_send, row_recv, pair_send, pair_recv, z_send, z_recv = sems
    near = at.unit
    started = []

    def go(src, send, recv, peer):
        copy = push(src, src, send, recv, peer)
        copy.start()
        started.append(copy)

    def landed(ref, send, recv, peer):
        push(ref, ref, send, recv, peer).wait_recv()

    def row_copy(act, which, k, slot, half, peer):
        act(half_of(out.at[slot], half), row_send.at[which, k], row_recv.at[which, k], peer)

    def to_rows(which, unit):
        mine = unit * n + at.row
        if at.square:
            row_copy(go, which, 0, mine, 0, at.side)
            row_copy(go, which, 1, mine, 1, at.over)
            row_copy(go, which, 2, mine, 1, at.side)
            row_copy(go, which, 3, mine, 0, at.over)
            return
        for s in range(1, n):
            go(out.at[mine], row_send.at[which, s], row_recv.at[which, s], (at.group, at.ahead(s)))

    def forward(which, unit):
        if at.square:
            side, over = unit * n + at.ring[1], unit * n + at.ring[2]
            row_copy(landed, which, 0, side, 0, at.side)
            row_copy(go, which, 4, side, 0, at.over)
            row_copy(landed, which, 1, over, 1, at.over)
            row_copy(go, which, 5, over, 1, at.side)

    def await_row(which, unit, s):
        slot = unit * n + at.behind(s)
        if not at.square:
            peer = (at.group, at.behind(s))
            landed(out.at[slot], row_send.at[which, s], row_recv.at[which, s], peer)
        elif s == 1:
            row_copy(landed, which, 2, slot, 1, at.side)
        elif s == 2:
            row_copy(landed, which, 3, slot, 0, at.over)
        else:
            row_copy(landed, which, 4, slot, 0, at.over)
            row_copy(landed, which, 5, slot, 1, at.side)

    def to_pair(which, s, unit):
        src = out.at[unit * n + at.behind(s)]
        go(src, pair_send.at[which, s], pair_recv.at[which, s], at.partner)

    def await_pair(which, s, unit):
        slot = (unit + 1 - 2 * at.core) * n + at.behind(s)
        landed(out.at[slot], pair_send.at[which, s], pair_recv.at[which, s], at.partner)
        use(slot)

    units = [near]
    if levels >= 2:
        units.append(lax.rem(near + 2, 4))
        go(out.at[near * n + at.row], z_send.at[0], z_recv.at[0], at.across)
    to_rows(0, near)
    if levels >= 1:
        to_pair(0, 0, near)
    if levels >= 2:
        landed(out.at[units[1] * n + at.row], z_send.at[0], z_recv.at[0], at.across)
        to_rows(1, units[1])
        to_pair(1, 0, units[1])
    use(near * n + at.row)
    if levels >= 2:
        use(units[1] * n + at.row)
    for which, unit in enumerate(units):
        forward(which, unit)
    for s in range(1, n):
        for which, unit in enumerate(units):
            await_row(which, unit, s)
            if levels >= 1:
                to_pair(which, s, unit)
                await_pair(which, s - 1, unit)
            use(unit * n + at.behind(s))
    if levels >= 1:
        for which, unit in enumerate(units):
            await_pair(which, n - 1, unit)
    for copy in started:
        copy.wait_send()


def solver(n, out, inverse_hbm, inverse, turned, total, sem):
    count, block, width = out.shape
    rows = inverse.shape[1]
    tile = min(rows, 256)
    whole = block % 128 == 0
    together = 1 if whole else turned.shape[0] // block
    copy = pltpu.make_async_copy(inverse_hbm, inverse, sem)
    copy.start()
    waiting = [copy]

    def multiply(slot, first):
        panel = out[slot] if whole else out[pl.ds(slot, together)].reshape(turned.shape)
        half = width // 2
        turned[:, :half] = -panel[:, half:]
        turned[:, half:] = panel[:, :half]
        span_columns = turned.shape[0]
        columns = pl.ds(pl.multiple_of(slot // together * span_columns, span_columns), span_columns)

        def body(index, carry):
            span = pl.ds(pl.multiple_of(index * tile, tile), tile)
            block_now = out[slot] if whole else panel
            real = jnp.dot(inverse[0, span, columns], block_now, preferred_element_type=jnp.float32)
            imag = jnp.dot(inverse[1, span, columns], turned[...], preferred_element_type=jnp.float32)
            if first:
                total[span, :] = real + imag
            else:
                total[span, :] = total[span, :] + (real + imag)
            return carry

        lax.fori_loop(0, rows // tile, body, 0)

    def use(slot):
        if whole:
            first = bool(waiting)
            if first:
                waiting.pop().wait()
            multiply(slot, first)

    def rest():
        if not whole:
            waiting.pop().wait()
            for slot in range(0, count, together):
                multiply(slot, slot == 0)

    return use, rest


def gather_kernel(n, levels, own, full, *sems):
    at = Place(n, levels)
    at.greet()
    full[at.unit * n + at.row] = own[...]
    spread(at, full, sems, lambda slot: None)


def gather_solve_kernel(n, levels, own, inverse_hbm, total, full, inverse, turned, sem, *sems):
    at = Place(n, levels)
    use, rest = solver(n, full, inverse_hbm, inverse, turned, total, sem)
    at.greet()
    full[at.unit * n + at.row] = own[...]
    spread(at, full, sems, use)
    rest()


def add_rows(out_ref, terms, panel=None):
    rows = out_ref.shape[0]
    step = min(rows, 64)

    def body(index, carry):
        span = pl.ds(pl.multiple_of(index * step, step), step)
        total = terms[0][span, :].astype(jnp.float32)
        for term in terms[1:]:
            total = total + term[span, :].astype(jnp.float32)
        if panel is not None:
            total = panel[span, :].astype(jnp.float32) - total
        out_ref[span, :] = total.astype(out_ref.dtype)
        return carry

    lax.fori_loop(0, rows // step, body, 0)


def reduce_solve_kernel(
    n, levels, term, panel, inverse_hbm, total, full, inverse, turned, near_buf, stage, row_buf, z_buf, sem, *sems
):
    at = Place(n, levels)
    halves = 2 ** (levels - 1)
    spread_sems = sems[:6]
    pair_send, pair_recv, row_send, row_recv, z_send, z_recv = sems[6:]
    use, finish_solve = solver(n, full, inverse_hbm, inverse, turned, total, sem)
    at.greet()
    started = []

    def go(src, dst, send, recv, peer):
        copy = push(src, dst, send, recv, peer)
        copy.start()
        started.append(copy)

    def landed(ref, send, recv, peer):
        push(ref, ref, send, recv, peer).wait_recv()

    order = [3, 1, 2, 0] if at.square else list(range(1, n)) + [0]
    for s in order:
        for half in range(halves):
            src = term.at[(half * 2 + 1 - at.core) * n + at.ahead(s)]
            go(src, near_buf.at[half, s], pair_send.at[half, s], pair_recv.at[half, s], at.partner)

    def own_term(half, s):
        return term.at[(half * 2 + at.core) * n + at.ahead(s)]

    def await_pair(half, s):
        landed(near_buf.at[half, s], pair_send.at[half, s], pair_recv.at[half, s], at.partner)

    def row_copy(half, k, src, peer):
        go(src, row_buf.at[half, k], row_send.at[half, k], row_recv.at[half, k], peer)

    def await_row(half, k, peer):
        landed(row_buf.at[half, k], row_send.at[half, k], row_recv.at[half, k], peer)

    if at.square:
        for half in range(halves):
            await_pair(half, 3)
            add_rows(stage.at[half, 3], [own_term(half, 3), near_buf.at[half, 3]])
            row_copy(half, 0, half_of(stage.at[half, 3], 0), at.side)
            row_copy(half, 3, half_of(stage.at[half, 3], 1), at.over)
        for half in range(halves):
            await_pair(half, 1)
            first = half_of(stage.at[half, 1], 0)
            add_rows(first, [half_of(own_term(half, 1), 0), half_of(near_buf.at[half, 1], 0)])
            row_copy(half, 1, first, at.side)
            await_pair(half, 2)
            second = half_of(stage.at[half, 2], 1)
            add_rows(second, [half_of(own_term(half, 2), 1), half_of(near_buf.at[half, 2], 1)])
            row_copy(half, 4, second, at.over)
        for half in range(halves):
            await_row(half, 0, at.side)
            first = half_of(stage.at[half, 2], 0)
            near = half_of(near_buf.at[half, 2], 0)
            add_rows(first, [half_of(own_term(half, 2), 0), near, row_buf.at[half, 0]])
            row_copy(half, 2, first, at.over)
            await_row(half, 3, at.over)
            second = half_of(stage.at[half, 1], 1)
            near = half_of(near_buf.at[half, 1], 1)
            add_rows(second, [half_of(own_term(half, 1), 1), near, row_buf.at[half, 3]])
            row_copy(half, 5, second, at.side)
        for half in range(halves):
            await_pair(half, 0)
            await_row(half, 1, at.side)
            await_row(half, 4, at.over)
            await_row(half, 2, at.over)
            await_row(half, 5, at.side)
    else:
        for s in range(1, n):
            for half in range(halves):
                await_pair(half, s)
                add_rows(stage.at[half, s], [own_term(half, s), near_buf.at[half, s]])
                row_copy(half, s, stage.at[half, s], (at.group, at.ahead(s)))
        for half in range(halves):
            await_pair(half, 0)
            for s in range(1, n):
                await_row(half, s, (at.group, at.behind(s)))

    def finish(dst, half, extra, base):
        own, near = own_term(half, 0), near_buf.at[half, 0]
        if not at.square:
            rest = [row_buf.at[half, s] for s in range(1, n)]
            add_rows(dst, [own, near] + rest + extra, base)
            return
        for part in range(2):
            rest = [row_buf.at[half, 1 + 3 * part], row_buf.at[half, 2 + 3 * part]]
            rest = rest + [half_of(ref, part) for ref in extra]
            terms = [half_of(own, part), half_of(near, part)] + rest
            add_rows(half_of(dst, part), terms, None if base is None else half_of(base, part))

    slot = at.unit * n + at.row
    if levels == 1:
        finish(full.at[slot], 0, [], panel)
    else:
        finish(z_buf.at[0], 1 - at.upper, [], None)
        go(z_buf.at[0], z_buf.at[1], z_send.at[0], z_recv.at[0], at.across)
        landed(z_buf.at[1], z_send.at[0], z_recv.at[0], at.across)
        finish(full.at[slot], at.upper, [z_buf.at[1]], panel)
    spread(at, full, spread_sems, use)
    finish_solve()
    for copy in started:
        copy.wait_send()


def dma(*shape):
    return pltpu.SemaphoreType.DMA(shape)


VMEM_SPEC = pl.BlockSpec(memory_space=pltpu.VMEM)
HBM_SPEC = pl.BlockSpec(memory_space=pl.ANY)


def spread_scratch(n):
    k = max(n, 6)
    return [dma(2, k), dma(2, k), dma(2, n), dma(2, n), dma(1), dma(1)]


def params(ident, mebibytes):
    return pltpu.CompilerParams(
        collective_id=ident, has_side_effects=True, vmem_limit_bytes=mebibytes << 20
    )


def gather(own, n, levels, ident):
    block, width = own.shape
    count = 2**levels * n
    full = pl.pallas_call(
        functools.partial(gather_kernel, n, levels),
        out_shape=jax.ShapeDtypeStruct((count, block, width), own.dtype),
        in_specs=[VMEM_SPEC],
        out_specs=VMEM_SPEC,
        scratch_shapes=spread_scratch(n),
        compiler_params=params(ident, 16),
    )(own)
    return full.reshape(count * block, width)


def solve_scratch(inverse, block, width, count):
    return [
        pltpu.VMEM((count, block, width), jnp.bfloat16),
        pltpu.VMEM(inverse.shape, inverse.dtype),
        pltpu.VMEM((block if block % 128 == 0 else 512, width), jnp.bfloat16),
    ]


def gather_solve(own, inverse, n, levels, ident):
    block, width = own.shape
    return pl.pallas_call(
        functools.partial(gather_solve_kernel, n, levels),
        out_shape=jax.ShapeDtypeStruct((inverse.shape[1], width), jnp.float32),
        in_specs=[VMEM_SPEC, HBM_SPEC],
        out_specs=VMEM_SPEC,
        scratch_shapes=solve_scratch(inverse, block, width, 2**levels * n)
        + [pltpu.SemaphoreType.DMA]
        + spread_scratch(n),
        compiler_params=params(ident, 32),
    )(own, inverse)


def reduce_solve(term, panel, inverse, n, levels, ident):
    block, width = panel.shape
    count = 2**levels * n
    halves = 2 ** (levels - 1)
    whole = pltpu.VMEM((halves, n, block, width), jnp.bfloat16)
    if n == 4:
        pieces, k = pltpu.VMEM((halves, 6, block // 2, width), jnp.bfloat16), 6
    else:
        pieces, k = whole, n
    return pl.pallas_call(
        functools.partial(reduce_solve_kernel, n, levels),
        out_shape=jax.ShapeDtypeStruct((inverse.shape[1], width), jnp.float32),
        in_specs=[VMEM_SPEC, VMEM_SPEC, HBM_SPEC],
        out_specs=VMEM_SPEC,
        scratch_shapes=solve_scratch(inverse, block, width, count)
        + [whole, whole, pieces, pltpu.VMEM((2, block, width), jnp.bfloat16)]
        + [pltpu.SemaphoreType.DMA]
        + spread_scratch(n)
        + [dma(halves, n), dma(halves, n), dma(halves, k), dma(halves, k), dma(1), dma(1)],
        compiler_params=params(ident, 32),
    )(term.reshape(count, block, width), panel, inverse)


def spread_rows(partial_rows, targets):
    marks = (lax.broadcasted_iota(jnp.int32, (F, 1), 0) == targets[None, :]).astype(jnp.bfloat16)
    return jnp.dot(
        marks, partial_rows.astype(jnp.bfloat16), preferred_element_type=jnp.float32
    ).astype(jnp.bfloat16)


def pick_rows(panel, targets):
    marks = (targets[:, None] == lax.broadcasted_iota(jnp.int32, (1, F), 1)).astype(jnp.bfloat16)
    return jnp.dot(marks, panel, preferred_element_type=jnp.float32).astype(jnp.bfloat16)


def on_device(
    n,
    panel_low,
    panel_mid,
    panel_top,
    inverse_low,
    inverse_mid,
    inverse_top,
    couple_low,
    couple_mid,
    parents_low,
    parents_mid,
):
    group = lax.axis_index("grp")
    low_targets = lax.dynamic_index_in_dim(parents_low, group, 0, keepdims=False)
    mid_targets = lax.dynamic_index_in_dim(parents_mid, group // 2, 0, keepdims=False)
    low_y = gather_solve(panel_low, inverse_low, n, 0, 0)
    term = spread_rows(complex_product(couple_low, low_y.astype(jnp.bfloat16)), low_targets)
    mid_y = reduce_solve(term, panel_mid, inverse_mid, n, 1, 1)
    term = spread_rows(complex_product(couple_mid, mid_y.astype(jnp.bfloat16)), mid_targets)
    top_x = reduce_solve(term, panel_top, inverse_top, n, 2, 2)
    top_full = gather(top_x.astype(jnp.bfloat16), n, 2, 3)
    lift = transposed_product(couple_mid, pick_rows(top_full, mid_targets)).astype(jnp.bfloat16)
    mid_x = mid_y - gather_solve(lift, inverse_mid, n, 1, 4)
    mid_full = gather(mid_x.astype(jnp.bfloat16), n, 1, 5)
    lift = transposed_product(couple_low, pick_rows(mid_full, low_targets)).astype(jnp.bfloat16)
    low_x = low_y - gather_solve(lift, inverse_low, n, 0, 6)
    return (low_x, mid_x, top_x)


def solution(mesh):
    placed = (
        P(("grp", "row"), None),
        P(("grp", "row"), None),
        P(("grp", "row"), None),
        P(None, ("grp", "row"), None),
        P(None, ("grp", "row"), None),
        P(None, ("grp", "row"), None),
        P(None, None, ("grp", "row")),
        P(None, None, ("grp", "row")),
        P(),
        P(),
    )
    return jax.shard_map(
        functools.partial(on_device, mesh.shape["row"]),
        mesh=mesh,
        in_specs=placed,
        out_specs=(P(("grp", "row"), None), P(("grp", "row"), None), P(("grp", "row"), None)),
        check_vma=False,
    )
```

```python
import functools

import jax
import jax.numpy as jnp
from jax import lax
from jax.experimental import pallas as pl
from jax.experimental.pallas import tpu as pltpu
from jax.sharding import PartitionSpec as P

F = 4096
MESH = pl.DeviceIdType.MESH


def complex_product(matrix, panel):
    width = panel.shape[1] // 2
    real_term = jnp.dot(matrix[0], panel, preferred_element_type=jnp.float32)
    imag_term = jnp.dot(matrix[1], panel, preferred_element_type=jnp.float32)
    return real_term + jnp.concatenate([-imag_term[:, width:], imag_term[:, :width]], axis=1)


def transposed_product(matrix, panel):
    width = panel.shape[1] // 2
    contract = (((0,), (0,)), ((), ()))
    real_term = lax.dot_general(matrix[0], panel, contract, preferred_element_type=jnp.float32)
    imag_term = lax.dot_general(matrix[1], panel, contract, preferred_element_type=jnp.float32)
    return real_term + jnp.concatenate([-imag_term[:, width:], imag_term[:, :width]], axis=1)


class Place:
    def __init__(self, n, levels):
        self.n = n
        self.levels = levels
        self.square = n == 4
        self.group = lax.axis_index("grp")
        self.row = lax.axis_index("row")
        self.core = lax.rem(self.group, 2)
        self.upper = lax.rem(self.group // 2, 2)
        self.partner = (self.group + 1 - 2 * self.core, self.row)
        self.across = (self.group + 2 - 4 * self.upper, self.row)
        self.unit = lax.rem(self.group, 2**levels)
        if self.square:
            side = self.row + 1 - 2 * lax.rem(self.row, 2)
            over = self.row + 2 - 4 * (self.row // 2)
            self.ring = [self.row, side, over, 3 - self.row]
            self.side = (self.group, side)
            self.over = (self.group, over)

    def ahead(self, step):
        return self.ring[step] if self.square else lax.rem(self.row + step, self.n)

    def behind(self, step):
        return self.ring[step] if self.square else lax.rem(self.row + self.n - step, self.n)

    def greet(self):
        barrier = pltpu.get_barrier_semaphore()
        if self.square:
            peers = [self.side, self.over]
        else:
            peers = [(self.group, self.ahead(s)) for s in range(1, self.n)]
        if self.levels >= 1:
            peers.append(self.partner)
        if self.levels >= 2:
            peers.append(self.across)
        for peer in peers:
            pl.semaphore_signal(barrier, inc=1, device_id=peer, device_id_type=MESH)
        pl.semaphore_wait(barrier, len(peers))


def push(src, dst, send, recv, peer):
    return pltpu.make_async_remote_copy(
        src_ref=src, dst_ref=dst, send_sem=send, recv_sem=recv, device_id=peer, device_id_type=MESH
    )


def half_of(ref, index):
    rows = ref.shape[0] // 2
    return ref.at[pl.ds(index * rows, rows)]


def spread(at, out, sems, use):
    n, levels = at.n, at.levels
    row_send, row_recv, pair_send, pair_recv, z_send, z_recv = sems
    near = at.unit
    started = []

    def go(src, send, recv, peer):
        copy = push(src, src, send, recv, peer)
        copy.start()
        started.append(copy)

    def landed(ref, send, recv, peer):
        push(ref, ref, send, recv, peer).wait_recv()

    def row_copy(act, which, k, slot, half, peer):
        act(half_of(out.at[slot], half), row_send.at[which, k], row_recv.at[which, k], peer)

    def to_rows(which, unit):
        mine = unit * n + at.row
        if at.square:
            row_copy(go, which, 0, mine, 0, at.side)
            row_copy(go, which, 1, mine, 1, at.over)
            row_copy(go, which, 2, mine, 1, at.side)
            row_copy(go, which, 3, mine, 0, at.over)
            return
        for s in range(1, n):
            go(out.at[mine], row_send.at[which, s], row_recv.at[which, s], (at.group, at.ahead(s)))

    def forward(which, unit):
        if at.square:
            side, over = unit * n + at.ring[1], unit * n + at.ring[2]
            row_copy(landed, which, 0, side, 0, at.side)
            row_copy(go, which, 4, side, 0, at.over)
            row_copy(landed, which, 1, over, 1, at.over)
            row_copy(go, which, 5, over, 1, at.side)

    def await_row(which, unit, s):
        slot = unit * n + at.behind(s)
        if not at.square:
            peer = (at.group, at.behind(s))
            landed(out.at[slot], row_send.at[which, s], row_recv.at[which, s], peer)
        elif s == 1:
            row_copy(landed, which, 2, slot, 1, at.side)
        elif s == 2:
            row_copy(landed, which, 3, slot, 0, at.over)
        else:
            row_copy(landed, which, 4, slot, 0, at.over)
            row_copy(landed, which, 5, slot, 1, at.side)

    def to_pair(which, s, unit):
        src = out.at[unit * n + at.behind(s)]
        go(src, pair_send.at[which, s], pair_recv.at[which, s], at.partner)

    def await_pair(which, s, unit):
        slot = (unit + 1 - 2 * at.core) * n + at.behind(s)
        landed(out.at[slot], pair_send.at[which, s], pair_recv.at[which, s], at.partner)
        use(slot)

    units = [near]
    if levels >= 2:
        units.append(lax.rem(near + 2, 4))
        go(out.at[near * n + at.row], z_send.at[0], z_recv.at[0], at.across)
    to_rows(0, near)
    if levels >= 1:
        to_pair(0, 0, near)
    if levels >= 2:
        landed(out.at[units[1] * n + at.row], z_send.at[0], z_recv.at[0], at.across)
        to_rows(1, units[1])
        to_pair(1, 0, units[1])
    use(near * n + at.row)
    if levels >= 2:
        use(units[1] * n + at.row)
    for which, unit in enumerate(units):
        forward(which, unit)
    for s in range(1, n):
        for which, unit in enumerate(units):
            await_row(which, unit, s)
            if levels >= 1:
                to_pair(which, s, unit)
                await_pair(which, s - 1, unit)
            use(unit * n + at.behind(s))
    if levels >= 1:
        for which, unit in enumerate(units):
            await_pair(which, n - 1, unit)
    for copy in started:
        copy.wait_send()


def solver(n, out, inverse_hbm, inverse, turned, total, sem):
    count, block, width = out.shape
    rows = inverse.shape[1]
    tile = min(rows, 256)
    whole = block % 128 == 0
    together = 1 if whole else turned.shape[0] // block
    copy = pltpu.make_async_copy(inverse_hbm, inverse, sem)
    copy.start()
    waiting = [copy]

    def multiply(slot, first):
        panel = out[slot] if whole else out[pl.ds(slot, together)].reshape(turned.shape)
        half = width // 2
        turned[:, :half] = -panel[:, half:]
        turned[:, half:] = panel[:, :half]
        span_columns = turned.shape[0]
        columns = pl.ds(pl.multiple_of(slot // together * span_columns, span_columns), span_columns)

        def body(index, carry):
            span = pl.ds(pl.multiple_of(index * tile, tile), tile)
            block_now = out[slot] if whole else panel
            real = jnp.dot(inverse[0, span, columns], block_now, preferred_element_type=jnp.float32)
            imag = jnp.dot(inverse[1, span, columns], turned[...], preferred_element_type=jnp.float32)
            if first:
                total[span, :] = real + imag
            else:
                total[span, :] = total[span, :] + (real + imag)
            return carry

        lax.fori_loop(0, rows // tile, body, 0)

    def use(slot):
        if whole:
            first = bool(waiting)
            if first:
                waiting.pop().wait()
            multiply(slot, first)

    def rest():
        if not whole:
            waiting.pop().wait()
            for slot in range(0, count, together):
                multiply(slot, slot == 0)

    return use, rest


def gather_kernel(n, levels, own, full, *sems):
    at = Place(n, levels)
    at.greet()
    full[at.unit * n + at.row] = own[...]
    spread(at, full, sems, lambda slot: None)


def gather_solve_kernel(n, levels, own, inverse_hbm, total, full, inverse, turned, sem, *sems):
    at = Place(n, levels)
    use, rest = solver(n, full, inverse_hbm, inverse, turned, total, sem)
    at.greet()
    full[at.unit * n + at.row] = own[...]
    spread(at, full, sems, use)
    rest()


def add_rows(out_ref, terms, panel=None):
    rows = out_ref.shape[0]
    step = min(rows, 64)

    def body(index, carry):
        span = pl.ds(pl.multiple_of(index * step, step), step)
        total = terms[0][span, :].astype(jnp.float32)
        for term in terms[1:]:
            total = total + term[span, :].astype(jnp.float32)
        if panel is not None:
            total = panel[span, :].astype(jnp.float32) - total
        out_ref[span, :] = total.astype(out_ref.dtype)
        return carry

    lax.fori_loop(0, rows // step, body, 0)


def reduce_solve_kernel(
    n, levels, term, panel, inverse_hbm, total, full, inverse, turned, near_buf, stage, row_buf, z_buf, sem, *sems
):
    at = Place(n, levels)
    halves = 2 ** (levels - 1)
    spread_sems = sems[:6]
    pair_send, pair_recv, row_send, row_recv, z_send, z_recv = sems[6:]
    use, finish_solve = solver(n, full, inverse_hbm, inverse, turned, total, sem)
    at.greet()
    started = []

    def go(src, dst, send, recv, peer):
        copy = push(src, dst, send, recv, peer)
        copy.start()
        started.append(copy)

    def landed(ref, send, recv, peer):
        push(ref, ref, send, recv, peer).wait_recv()

    order = [3, 1, 2, 0] if at.square else list(range(1, n)) + [0]
    for s in order:
        for half in range(halves):
            src = term.at[(half * 2 + 1 - at.core) * n + at.ahead(s)]
            go(src, near_buf.at[half, s], pair_send.at[half, s], pair_recv.at[half, s], at.partner)

    def own_term(half, s):
        return term.at[(half * 2 + at.core) * n + at.ahead(s)]

    def await_pair(half, s):
        landed(near_buf.at[half, s], pair_send.at[half, s], pair_recv.at[half, s], at.partner)

    def row_copy(half, k, src, peer):
        go(src, row_buf.at[half, k], row_send.at[half, k], row_recv.at[half, k], peer)

    def await_row(half, k, peer):
        landed(row_buf.at[half, k], row_send.at[half, k], row_recv.at[half, k], peer)

    if at.square:
        for half in range(halves):
            await_pair(half, 3)
            add_rows(stage.at[half, 3], [own_term(half, 3), near_buf.at[half, 3]])
            row_copy(half, 0, half_of(stage.at[half, 3], 0), at.side)
            row_copy(half, 3, half_of(stage.at[half, 3], 1), at.over)
        for half in range(halves):
            await_pair(half, 1)
            first = half_of(stage.at[half, 1], 0)
            add_rows(first, [half_of(own_term(half, 1), 0), half_of(near_buf.at[half, 1], 0)])
            row_copy(half, 1, first, at.side)
            await_pair(half, 2)
            second = half_of(stage.at[half, 2], 1)
            add_rows(second, [half_of(own_term(half, 2), 1), half_of(near_buf.at[half, 2], 1)])
            row_copy(half, 4, second, at.over)
        for half in range(halves):
            await_row(half, 0, at.side)
            first = half_of(stage.at[half, 2], 0)
            near = half_of(near_buf.at[half, 2], 0)
            add_rows(first, [half_of(own_term(half, 2), 0), near, row_buf.at[half, 0]])
            row_copy(half, 2, first, at.over)
            await_row(half, 3, at.over)
            second = half_of(stage.at[half, 1], 1)
            near = half_of(near_buf.at[half, 1], 1)
            add_rows(second, [half_of(own_term(half, 1), 1), near, row_buf.at[half, 3]])
            row_copy(half, 5, second, at.side)
        for half in range(halves):
            await_pair(half, 0)
            await_row(half, 1, at.side)
            await_row(half, 4, at.over)
            await_row(half, 2, at.over)
            await_row(half, 5, at.side)
    else:
        for s in range(1, n):
            for half in range(halves):
                await_pair(half, s)
                add_rows(stage.at[half, s], [own_term(half, s), near_buf.at[half, s]])
                row_copy(half, s, stage.at[half, s], (at.group, at.ahead(s)))
        for half in range(halves):
            await_pair(half, 0)
            for s in range(1, n):
                await_row(half, s, (at.group, at.behind(s)))

    def finish(dst, half, extra, base):
        own, near = own_term(half, 0), near_buf.at[half, 0]
        if not at.square:
            rest = [row_buf.at[half, s] for s in range(1, n)]
            add_rows(dst, [own, near] + rest + extra, base)
            return
        for part in range(2):
            rest = [row_buf.at[half, 1 + 3 * part], row_buf.at[half, 2 + 3 * part]]
            rest = rest + [half_of(ref, part) for ref in extra]
            terms = [half_of(own, part), half_of(near, part)] + rest
            add_rows(half_of(dst, part), terms, None if base is None else half_of(base, part))

    slot = at.unit * n + at.row
    if levels == 1:
        finish(full.at[slot], 0, [], panel)
    else:
        finish(z_buf.at[0], 1 - at.upper, [], None)
        go(z_buf.at[0], z_buf.at[1], z_send.at[0], z_recv.at[0], at.across)
        landed(z_buf.at[1], z_send.at[0], z_recv.at[0], at.across)
        finish(full.at[slot], at.upper, [z_buf.at[1]], panel)
    spread(at, full, spread_sems, use)
    finish_solve()
    for copy in started:
        copy.wait_send()


def dma(*shape):
    return pltpu.SemaphoreType.DMA(shape)


VMEM_SPEC = pl.BlockSpec(memory_space=pltpu.VMEM)
HBM_SPEC = pl.BlockSpec(memory_space=pltpu.HBM)


def spread_scratch(n):
    k = max(n, 6)
    return [dma(2, k), dma(2, k), dma(2, n), dma(2, n), dma(1), dma(1)]


def params(ident, mebibytes):
    return pltpu.CompilerParams(
        collective_id=ident, has_side_effects=True, vmem_limit_bytes=mebibytes << 20
    )


def gather(own, n, levels, ident):
    block, width = own.shape
    count = 2**levels * n
    full = pl.pallas_call(
        functools.partial(gather_kernel, n, levels),
        out_shape=jax.ShapeDtypeStruct((count, block, width), own.dtype),
        in_specs=[VMEM_SPEC],
        out_specs=VMEM_SPEC,
        scratch_shapes=spread_scratch(n),
        compiler_params=params(ident, 16),
    )(own)
    return full.reshape(count * block, width)


def solve_scratch(inverse, block, width, count):
    return [
        pltpu.VMEM((count, block, width), jnp.bfloat16),
        pltpu.VMEM(inverse.shape, inverse.dtype),
        pltpu.VMEM((block if block % 128 == 0 else 512, width), jnp.bfloat16),
    ]


def gather_solve(own, inverse, n, levels, ident):
    block, width = own.shape
    return pl.pallas_call(
        functools.partial(gather_solve_kernel, n, levels),
        out_shape=jax.ShapeDtypeStruct((inverse.shape[1], width), jnp.float32),
        in_specs=[VMEM_SPEC, HBM_SPEC],
        out_specs=VMEM_SPEC,
        scratch_shapes=solve_scratch(inverse, block, width, 2**levels * n)
        + [pltpu.SemaphoreType.DMA]
        + spread_scratch(n),
        compiler_params=params(ident, 32),
    )(own, inverse)


def reduce_solve(term, panel, inverse, n, levels, ident):
    block, width = panel.shape
    count = 2**levels * n
    halves = 2 ** (levels - 1)
    whole = pltpu.VMEM((halves, n, block, width), jnp.bfloat16)
    if n == 4:
        pieces, k = pltpu.VMEM((halves, 6, block // 2, width), jnp.bfloat16), 6
    else:
        pieces, k = whole, n
    return pl.pallas_call(
        functools.partial(reduce_solve_kernel, n, levels),
        out_shape=jax.ShapeDtypeStruct((inverse.shape[1], width), jnp.float32),
        in_specs=[VMEM_SPEC, VMEM_SPEC, HBM_SPEC],
        out_specs=VMEM_SPEC,
        scratch_shapes=solve_scratch(inverse, block, width, count)
        + [whole, whole, pieces, pltpu.VMEM((2, block, width), jnp.bfloat16)]
        + [pltpu.SemaphoreType.DMA]
        + spread_scratch(n)
        + [dma(halves, n), dma(halves, n), dma(halves, k), dma(halves, k), dma(1), dma(1)],
        compiler_params=params(ident, 32),
    )(term.reshape(count, block, width), panel, inverse)


def spread_kernel(tile, targets, rows, out):
    index = lax.broadcasted_iota(jnp.int32, (tile, 1), 0) + pl.program_id(0) * tile
    marks = (index == targets[...]).astype(jnp.float32).astype(jnp.bfloat16)
    out[...] = jnp.dot(marks, rows[...], preferred_element_type=jnp.float32).astype(out.dtype)


def spread_rows(partial_rows, targets):
    count, width = partial_rows.shape
    tile = F // 4
    return pl.pallas_call(
        functools.partial(spread_kernel, tile),
        grid=(F // tile,),
        in_specs=[
            pl.BlockSpec((1, count), lambda i: (0, 0)),
            pl.BlockSpec((count, width), lambda i: (0, 0)),
        ],
        out_specs=pl.BlockSpec((tile, width), lambda i: (i, 0)),
        out_shape=jax.ShapeDtypeStruct((F, width), jnp.bfloat16),
        compiler_params=pltpu.CompilerParams(vmem_limit_bytes=32 << 20),
    )(targets[None, :], partial_rows.astype(jnp.bfloat16))


def pick_rows(panel, targets):
    marks = (targets[:, None] == lax.broadcasted_iota(jnp.int32, (1, F), 1)).astype(jnp.bfloat16)
    return jnp.dot(marks, panel, preferred_element_type=jnp.float32).astype(jnp.bfloat16)


def on_device(
    n,
    panel_low,
    panel_mid,
    panel_top,
    inverse_low,
    inverse_mid,
    inverse_top,
    couple_low,
    couple_mid,
    parents_low,
    parents_mid,
):
    group = lax.axis_index("grp")
    low_targets = lax.dynamic_index_in_dim(parents_low, group, 0, keepdims=False)
    mid_targets = lax.dynamic_index_in_dim(parents_mid, group // 2, 0, keepdims=False)
    low_y = gather_solve(panel_low, inverse_low, n, 0, 0)
    term = spread_rows(complex_product(couple_low, low_y.astype(jnp.bfloat16)), low_targets)
    mid_y = reduce_solve(term, panel_mid, inverse_mid, n, 1, 1)
    term = spread_rows(complex_product(couple_mid, mid_y.astype(jnp.bfloat16)), mid_targets)
    top_x = reduce_solve(term, panel_top, inverse_top, n, 2, 2)
    top_full = gather(top_x.astype(jnp.bfloat16), n, 2, 3)
    lift = transposed_product(couple_mid, pick_rows(top_full, mid_targets)).astype(jnp.bfloat16)
    mid_x = mid_y - gather_solve(lift, inverse_mid, n, 1, 4)
    mid_full = gather(mid_x.astype(jnp.bfloat16), n, 1, 5)
    lift = transposed_product(couple_low, pick_rows(mid_full, low_targets)).astype(jnp.bfloat16)
    low_x = low_y - gather_solve(lift, inverse_low, n, 0, 6)
    return (low_x, mid_x, top_x)


def solution(mesh):
    placed = (
        P(("grp", "row"), None),
        P(("grp", "row"), None),
        P(("grp", "row"), None),
        P(None, ("grp", "row"), None),
        P(None, ("grp", "row"), None),
        P(None, ("grp", "row"), None),
        P(None, None, ("grp", "row")),
        P(None, None, ("grp", "row")),
        P(),
        P(),
    )
    return jax.shard_map(
        functools.partial(on_device, mesh.shape["row"]),
        mesh=mesh,
        in_specs=placed,
        out_specs=(P(("grp", "row"), None), P(("grp", "row"), None), P(("grp", "row"), None)),
        check_vma=False,
    )
```
